32 devices in a mesh: grp: 2 (over x), row: 2 (over core), col: 8 (over z, y).
Axes of the slice: x: 2, y: 2, z: 4, core: 2. Of those that a mesh axis runs over, the one named last changes fastest.
Arguments:
- hidden_acts: bfloat16 [512, 26624], P(('grp', 'row'), 'col'), parts along dimension 0, may hold values from -216 to 216
- down_weight: bfloat16 [26624, 8192], P('col', 'row'), may hold values from -0.0390625 to 0.0390625
- amax_history: float32 [8], P('grp'), parts along dimension 0, may hold values from 3 to 12
Outputs:
- scaled_out: bfloat16 [512, 8192], P(('grp', 'col'), 'row'), parts along dimension 0
- token_scale: float32 [512], P(('grp', 'row')), parts along dimension 0
- history_next: float32 [8], P('grp'), parts along dimension 0
The draws below stay inside these ranges and needn't reach their ends.
There are 2 independent parts, one for each index of `grp`. The reference program is written for one: setup_inputs(seed, part) draws one part's arguments, and reference() takes and returns one part's arrays. A program takes and returns all parts, laid end to end along the dimension named above; an argument that names none is the same for every part. Nothing has to cross between parts.
All inputs are finite; a program needn't handle non-finite values.
Results may differ from the reference program's by a relative error of at most 0.0044.
Values may be sent and summed in bfloat16 or wider, within the bound.
No kernel may reach another device: no remote copies, remote signals or barrier semaphores. Data moves between devices by JAX's collectives and lax.ppermute only.
A program may use at most 64 MiB of HBM per device.

```python
import math
import jax
import jax.numpy as jnp
from jax import lax

D = 8192
F = 26624
HIST = 4
TOKENS_BLK = 32
TOKENS = 256
F_BLK = 3328


def draw_hidden_acts(key, part):
    key_vals = jax.random.fold_in(key, 11)
    key_rows = jax.random.fold_in(key, 12)
    key_cols = jax.random.fold_in(key, 13)
    key_order = jax.random.fold_in(key, 14)
    key_place = jax.random.fold_in(key, 15)
    key_where = jax.random.fold_in(key, 16)
    key_signs = jax.random.fold_in(key, 17)
    key_heavy = jax.random.fold_in(key, 18)
    key_posit = jax.random.fold_in(key, 19)
    blocks = TOKENS // TOKENS_BLK
    quiet_count = max(1, blocks // 4)
    values = jnp.clip(jax.random.normal(key_vals, (TOKENS, F), jnp.float32), -6.0, 6.0)
    row_spread = math.log(4.0)
    order = jax.random.permutation(key_order, blocks)
    quiet_blocks = order[:quiet_count]
    heavy_block = order[quiet_count]
    block_of_row = jnp.arange(TOKENS, dtype=jnp.int32) // TOKENS_BLK
    quiet_row = jnp.any(block_of_row[:, None] == quiet_blocks[None, :], axis=1)
    heavy_index = heavy_block * TOKENS_BLK + jax.random.randint(key_heavy, (), 0, TOKENS_BLK)
    heavy_row = jnp.arange(TOKENS, dtype=jnp.int32) == heavy_index
    row_pos = jax.random.permutation(key_posit, TOKENS).astype(jnp.float32) / TOKENS
    col_pos = jnp.arange(F, dtype=jnp.float32) / F
    row_scale = jnp.exp(math.log(3.0) * row_pos + jax.random.uniform(key_rows, (TOKENS,), jnp.float32, 0.0, row_spread))
    row_scale = row_scale * jnp.where(heavy_row, 1.5, 1.0) * jnp.where(quiet_row, 0.1, 1.0)
    col_scale = jnp.exp(math.log(3.0) * col_pos + jax.random.uniform(key_cols, (F,), jnp.float32, 0.0, math.log(4.0)))
    base = 0.15 * values * row_scale[:, None] * col_scale[None, :]
    spike_rows = quiet_blocks * TOKENS_BLK + jax.random.randint(key_place, (quiet_count,), 0, TOKENS_BLK)
    spike_cols = jax.random.randint(key_where, (quiet_count,), 0, F)
    spike_signs = jnp.where(jax.random.randint(key_signs, (quiet_count,), 0, 2) == 0, -216.0, 216.0).astype(jnp.float32)
    base = base.at[spike_rows, spike_cols].set(spike_signs)
    return base.astype(jnp.bfloat16)


def block_scale(stream_key, shape, cuts, low, top_value):
    factor_of, own = 1.0, jax.random.fold_in(stream_key, 6)
    for axis_at, shards_of in cuts:
        heights = jnp.exp(jax.random.uniform(jax.random.fold_in(own, axis_at), (shards_of,), jnp.float32, low / len(cuts), top_value / len(cuts)))
        factor_of = factor_of * jnp.repeat(heights, shape[axis_at] // shards_of).reshape([-1 if axis == axis_at else 1 for axis in range(len(shape))])
    return factor_of


def bell_draw(own_key, dims, scale, reach, pieces=(), kind=jnp.bfloat16):
    entries = scale * jax.random.normal(own_key, dims, jnp.float32)
    if pieces:
        entries = entries * block_scale(own_key, dims, pieces, -0.22, 0.18)
    return jnp.clip(entries, -reach, reach).astype(kind)


def setup_inputs(seed: int = 0, part: int = 0) -> dict:
    seeds = jax.random.split(jax.random.key(seed), 4)
    part_keys = jax.random.split(jax.random.fold_in(seeds[3], part), 4)
    hidden_acts = draw_hidden_acts(jax.random.fold_in(jax.random.fold_in(seeds[3], part), 71), part)
    down_weight = bell_draw(seeds[1], (F, D), F ** -0.5, 0.0390625, ((0, 8), (1, 2)))
    amax_history = jnp.clip(jnp.exp(jax.random.uniform(part_keys[2], (HIST,), jnp.float32, math.log(3.0), math.log(12.0))), 3.0, 12.0)
    return {"hidden_acts": hidden_acts, "down_weight": down_weight, "amax_history": amax_history}


clip_ratio = 0.5
format_limit = 448.0


def reference(hidden_acts, down_weight, amax_history):
    peak_tok = jnp.max(jnp.abs(hidden_acts), axis=1).astype(jnp.float32)
    token_scale = clip_ratio * (peak_tok + 1e-6) / format_limit
    quantized = jnp.clip(hidden_acts.astype(jnp.float32) / token_scale[:, None], -format_limit, format_limit).astype(jnp.bfloat16)
    blocks = F // F_BLK
    quant_blocks = jnp.transpose(quantized.reshape(TOKENS, blocks, F_BLK), (1, 0, 2))
    weight_blocks = down_weight.reshape(blocks, F_BLK, D)

    def add_block(total, pair):
        quant_part, weight_part = pair
        partial_value = jnp.dot(quant_part, weight_part, preferred_element_type=jnp.float32)
        return total + partial_value, None

    summed, _ = lax.scan(add_block, jnp.zeros((TOKENS, D), jnp.float32), (quant_blocks, weight_blocks))
    result = summed * token_scale[:, None]
    previous = jnp.max(amax_history)
    scaled_out = jnp.clip(result / previous, -1.0, 1.0).astype(jnp.bfloat16)
    newest = jnp.max(jnp.abs(result))
    history_next = jnp.concatenate([newest[None], amax_history[:-1]])
    return scaled_out, token_scale, history_next
```

```python
import functools

import jax
import jax.numpy as jnp
from jax import lax
from jax.experimental import pallas as pl
from jax.experimental.pallas import tpu as pltpu
from jax.sharding import PartitionSpec as P

clip_ratio = 0.5
format_limit = 448.0
CHUNKS = 4


def prepare_body(place, own_ref, other_ref, scale_ref, out_ref):
    step = pl.program_id(0)
    block, mine = place[0, step], place[1, step]
    size = out_ref.shape[0]
    start = pl.multiple_of(block * size, size)
    own = own_ref[pl.ds(start, size), :].astype(jnp.float32)
    other = other_ref[pl.ds(start, size), :].astype(jnp.float32)
    values = jnp.where(mine == 1, own, other)
    inverse = 1.0 / scale_ref[...]
    out_ref[...] = jnp.clip(values * inverse, -format_limit, format_limit).astype(
        jnp.bfloat16
    )


def prepare(own, other, scales, place, blocks):
    rows, depth = own.shape
    size = 2 * rows // blocks
    return pl.pallas_call(
        prepare_body,
        out_shape=jax.ShapeDtypeStruct((2 * rows, depth), jnp.bfloat16),
        grid_spec=pltpu.PrefetchScalarGridSpec(
            num_scalar_prefetch=1,
            grid=(blocks,),
            in_specs=[
                pl.BlockSpec((rows, depth), lambda i, place: (0, 0)),
                pl.BlockSpec((rows, depth), lambda i, place: (0, 0)),
                pl.BlockSpec((size, 1), lambda i, place: (place[2, i], 0)),
            ],
            out_specs=pl.BlockSpec((size, depth), lambda i, place: (i, 0)),
        ),
        compiler_params=pltpu.CompilerParams(vmem_limit_bytes=16 << 20),
        cost_estimate=pl.CostEstimate(
            flops=6 * rows * depth, bytes_accessed=8 * rows * depth, transcendentals=0
        ),
        name="prepare",
    )(place, own, other, scales)


def product_body(first, tile, lhs_ref, weight_ref, keep_ref, send_ref):
    width = keep_ref.shape[1]
    half = keep_ref.shape[0]

    @pl.loop(0, width // tile)
    def _(step):
        at = pl.multiple_of(step * tile, tile)
        out = jnp.dot(
            lhs_ref[...],
            weight_ref[:, pl.ds(pl.multiple_of(first + at, tile), tile)],
            preferred_element_type=jnp.float32,
        )
        keep_ref[:, pl.ds(at, tile)] = out[:half]
        send_ref[:, pl.ds(at, tile)] = out[half:].astype(jnp.bfloat16)


def product(lhs, weight, first, width):
    rows, depth = lhs.shape
    tile = min(512, width)
    return pl.pallas_call(
        functools.partial(product_body, first, tile),
        out_shape=(
            jax.ShapeDtypeStruct((rows // 2, width), jnp.float32),
            jax.ShapeDtypeStruct((rows // 2, width), jnp.bfloat16),
        ),
        in_specs=[pl.BlockSpec(memory_space=pltpu.VMEM)] * 2,
        out_specs=(pl.BlockSpec(memory_space=pltpu.VMEM),) * 2,
        compiler_params=pltpu.CompilerParams(vmem_limit_bytes=20 << 20),
        cost_estimate=pl.CostEstimate(
            flops=2 * rows * depth * width,
            bytes_accessed=2 * depth * width,
            transcendentals=0,
        ),
        name="product",
    )(lhs, weight)


def on_device(hidden_acts, down_weight, amax_history):
    cols = lax.axis_size("col")
    bits = cols.bit_length() - 1
    col, row = lax.axis_index("col"), lax.axis_index("row")
    rows, depth = hidden_acts.shape
    block = 2 * rows // cols
    orders = [list(range(bits)), list(range(bits))]
    if bits > 1:
        orders[1][:2] = [1, 0]

    def across(value, flips):
        pairs = []
        for r in range(2):
            for c in range(cols):
                dr, dc = flips[r]
                pairs.append((r * cols + c, (r ^ dr) * cols + (c ^ dc)))
        return lax.ppermute(value, ("row", "col"), pairs)

    def both(dr, dc):
        return ((dr, dc), (dr, dc))

    weight = pltpu.with_memory_space_constraint(down_weight, pltpu.VMEM)
    other_acts = across(hidden_acts, both(1, 0))
    peak = jnp.max(jnp.abs(hidden_acts), axis=1).astype(jnp.float32)
    for bit in range(bits):
        peak = jnp.maximum(peak, across(peak, both(0, 1 << bit)))
    own_scale = clip_ratio * (peak + 1e-06) / format_limit
    other_scale = across(own_scale, both(1, 0))
    all_scale = jnp.where(
        row == 0,
        jnp.concatenate([own_scale, other_scale]),
        jnp.concatenate([other_scale, own_scale]),
    )

    member = []
    for order in orders:
        member.append(
            [
                sum(((q >> (bits - 1 - j)) & 1) << bit for j, bit in enumerate(order))
                for q in range(cols)
            ]
        )
    wanted = col ^ jnp.where(
        row == 0, jnp.array(member[0], jnp.int32), jnp.array(member[1], jnp.int32)
    )
    half = cols // 2
    place = jnp.stack(
        [wanted % half, (wanted // half == row).astype(jnp.int32), wanted]
    )
    lhs = prepare(hidden_acts, other_acts, all_scale[:, None], place, cols)

    width = down_weight.shape[1] // CHUNKS
    sums = []
    for chunk in range(CHUNKS):
        keep, send = product(lhs, weight, chunk * width, width)
        for stage in range(bits):
            flips = tuple((0, 1 << orders[r][stage]) for r in range(2))
            got = across(send, flips)
            total = keep + got.astype(jnp.float32)
            middle = total.shape[0] // 2
            if stage < bits - 1:
                keep, send = total[:middle], total[middle:].astype(jnp.bfloat16)
        sums.append(total)

    previous = jnp.max(amax_history)
    block_scale = lax.dynamic_slice_in_dim(all_scale, col * block, block)[:, None]
    results = [part * block_scale for part in sums]
    newest = functools.reduce(
        jnp.maximum, [jnp.max(jnp.abs(part)) for part in results]
    )[None]
    newest = jnp.maximum(newest, across(newest, both(1, 0)))
    for bit in range(bits):
        newest = jnp.maximum(newest, across(newest, both(0, 1 << bit)))
    scaled_out = jnp.concatenate(
        [jnp.clip(part / previous, -1.0, 1.0).astype(jnp.bfloat16) for part in results],
        axis=1,
    )
    history_next = jnp.concatenate([newest, amax_history[:-1]])
    return (scaled_out, own_scale, history_next)


def solution(mesh):
    in_specs = (P(("grp", "row"), "col"), P("col", "row"), P("grp"))
    out_specs = (P(("grp", "col"), "row"), P(("grp", "row")), P("grp"))
    return jax.shard_map(
        on_device, mesh=mesh, in_specs=in_specs, out_specs=out_specs, check_vma=False
    )
```

```python
import functools

import jax
import jax.numpy as jnp
from jax import lax
from jax.experimental import pallas as pl
from jax.experimental.pallas import tpu as pltpu
from jax.sharding import PartitionSpec as P


clip_ratio = 0.5
format_limit = 448.0
EIGHTHS = (1, 2, 2, 3)
GROUPS = ((0, 1), (2, 3))


def orders_of(bits):
    orders = [list(range(bits)), list(range(bits))]
    if bits > 1:
        orders[1][:2] = [1, 0]
    return orders


def matmul(lhs_ref, weight_ref, keep_ref, send_ref):
    half, width = keep_ref.shape
    tile = min(512, width)

    @pl.loop(0, width // tile)
    def _(step):
        at = pl.ds(pl.multiple_of(step * tile, tile), tile)
        out = jnp.dot(
            lhs_ref[...], weight_ref[:, at], preferred_element_type=jnp.float32
        )
        keep_ref[:, at] = out[:half]
        send_ref[:, at] = out[half:].astype(jnp.bfloat16)


def first_body(
    cols,
    own_hbm,
    other_ref,
    own_scale,
    other_scale,
    weight_hbm,
    lhs_ref,
    keep_ref,
    send_ref,
    next_ref,
    own_ref,
    weight_ref,
    sems,
):
    bits = cols.bit_length() - 1
    orders = orders_of(bits)
    col, row = lax.axis_index("col"), lax.axis_index("row")
    half = cols // 2
    size = lhs_ref.shape[0] // cols
    width, after = weight_ref.shape[1], next_ref.shape[1]
    own_copy = pltpu.make_async_copy(own_hbm, own_ref, sems.at[0])
    own_copy.start()
    now = pltpu.make_async_copy(weight_hbm.at[:, :width], weight_ref, sems.at[1])
    now.start()

    def position(block):
        away = block ^ col
        where = [
            sum(((away >> bit) & 1) << (bits - 1 - j) for j, bit in enumerate(order))
            for order in orders
        ]
        return jnp.where(row == 0, where[0], where[1])

    def quantize(acts_ref, scale_ref, owner):
        @pl.loop(0, half)
        def _(step):
            at = pl.ds(pl.multiple_of(step * size, size), size)
            to = pl.ds(pl.multiple_of(position(owner * half + step) * size, size), size)
            inverse = 1.0 / scale_ref[at, :]
            values = acts_ref[at, :].astype(jnp.float32) * inverse
            lhs_ref[to, :] = jnp.clip(values, -format_limit, format_limit).astype(
                jnp.bfloat16
            )

    quantize(other_ref, other_scale, 1 - row)
    own_copy.wait()
    later = pltpu.make_async_copy(
        weight_hbm.at[:, width : width + after], next_ref, sems.at[2]
    )
    later.start()
    quantize(own_ref, own_scale, row)
    now.wait()
    matmul(lhs_ref, weight_ref, keep_ref, send_ref)
    later.wait()


def middle_body(
    begin, lhs_ref, weight_ref, weight_hbm, keep_ref, send_ref, next_ref, sem
):
    after = next_ref.shape[1]
    later = pltpu.make_async_copy(
        weight_hbm.at[:, begin : begin + after], next_ref, sem
    )
    later.start()
    matmul(lhs_ref, weight_ref, keep_ref, send_ref)
    later.wait()


def last_body(lhs_ref, weight_ref, keep_ref, send_ref):
    matmul(lhs_ref, weight_ref, keep_ref, send_ref)


def finish_body(history, keep_ref, got_ref, scale_ref, out_ref, peak_ref):
    result = (keep_ref[...] + got_ref[...].astype(jnp.float32)) * scale_ref[...]
    previous = history[0]
    for at in range(1, history.shape[0]):
        previous = jnp.maximum(previous, history[at])
    out_ref[...] = jnp.clip(result / previous, -1.0, 1.0).astype(jnp.bfloat16)
    peak_ref[...] = jnp.full(peak_ref.shape, jnp.max(jnp.abs(result)), jnp.float32)


VMEM = pl.BlockSpec(memory_space=pltpu.VMEM)
SMEM = pl.BlockSpec(memory_space=pltpu.SMEM)
HBM = pl.BlockSpec(memory_space=pltpu.HBM)


def products(own, other, own_scale, other_scale, weight, cols):
    rows, depth = own.shape
    total = 2 * rows
    widths = [weight.shape[1] * part // sum(EIGHTHS) for part in EIGHTHS]
    pair = lambda width: (
        jax.ShapeDtypeStruct((total // 2, width), jnp.float32),
        jax.ShapeDtypeStruct((total // 2, width), jnp.bfloat16),
    )
    piece = lambda width: pltpu.VMEM((depth, width), jnp.bfloat16)
    params = pltpu.CompilerParams(vmem_limit_bytes=12 << 20)
    cost = lambda width: pl.CostEstimate(
        flops=2 * total * depth * width,
        bytes_accessed=2 * depth * width,
        transcendentals=0,
    )
    lhs, *first, held = pl.pallas_call(
        functools.partial(first_body, cols),
        out_shape=(
            jax.ShapeDtypeStruct((total, depth), jnp.bfloat16),
            *pair(widths[0]),
            piece(widths[1]),
        ),
        in_specs=[HBM, VMEM, VMEM, VMEM, HBM],
        out_specs=(VMEM,) * 4,
        scratch_shapes=[
            pltpu.VMEM((rows, depth), jnp.bfloat16),
            pltpu.VMEM((depth, widths[0]), jnp.bfloat16),
            pltpu.SemaphoreType.DMA((3,)),
        ],
        compiler_params=params,
        cost_estimate=cost(widths[0]),
        name="first",
    )(own, other, own_scale, other_scale, weight)
    made = [first]
    begin = widths[0]
    for at in range(1, len(widths)):
        begin += widths[at]
        if at + 1 < len(widths):
            *part, held = pl.pallas_call(
                functools.partial(middle_body, begin),
                out_shape=(*pair(widths[at]), piece(widths[at + 1])),
                in_specs=[VMEM, VMEM, HBM],
                out_specs=(VMEM,) * 3,
                scratch_shapes=[pltpu.SemaphoreType.DMA],
                compiler_params=params,
                cost_estimate=cost(widths[at]),
                name="middle",
            )(lhs, held, weight)
        else:
            part = pl.pallas_call(
                last_body,
                out_shape=pair(widths[at]),
                in_specs=[VMEM, VMEM],
                out_specs=(VMEM,) * 2,
                compiler_params=params,
                cost_estimate=cost(widths[at]),
                name="last",
            )(lhs, held)
        made.append(part)
    return made


def finish(keep, got, scale, history):
    return pl.pallas_call(
        finish_body,
        out_shape=(
            jax.ShapeDtypeStruct(keep.shape, jnp.bfloat16),
            jax.ShapeDtypeStruct((8, 128), jnp.float32),
        ),
        in_specs=[SMEM, VMEM, VMEM, VMEM],
        out_specs=(VMEM, VMEM),
        compiler_params=pltpu.CompilerParams(vmem_limit_bytes=8 << 20),
        cost_estimate=pl.CostEstimate(
            flops=6 * keep.size, bytes_accessed=6 * keep.size, transcendentals=0
        ),
        name="finish",
    )(history, keep, got, scale)


def on_device(hidden_acts, down_weight, amax_history):
    cols = lax.axis_size("col")
    bits = cols.bit_length() - 1
    orders = orders_of(bits)
    col, row = lax.axis_index("col"), lax.axis_index("row")
    block = 2 * hidden_acts.shape[0] // cols

    def across(value, flips):
        pairs = []
        for r in range(2):
            for c in range(cols):
                dr, dc = flips[r]
                pairs.append((r * cols + c, (r ^ dr) * cols + (c ^ dc)))
        return lax.ppermute(value, ("row", "col"), pairs)

    def both(dr, dc):
        return ((dr, dc), (dr, dc))

    def stage(value, at):
        return across(value, tuple((0, 1 << orders[r][at]) for r in range(2)))

    other_acts = across(hidden_acts, both(1, 0))
    peak = jnp.max(jnp.abs(hidden_acts), axis=1).astype(jnp.float32)
    for bit in range(bits):
        peak = jnp.maximum(peak, across(peak, both(0, 1 << bit)))
    own_scale = clip_ratio * (peak + 1e-06) / format_limit
    other_scale = across(own_scale, both(1, 0))

    made = products(
        hidden_acts, other_acts, own_scale[:, None], other_scale[:, None], down_weight, cols
    )
    totals = []
    for keep, send in made:
        got = stage(send, 0)
        totals.append(keep + got.astype(jnp.float32))

    mine = lax.dynamic_slice_in_dim(
        jnp.where(
            row == 0,
            jnp.concatenate([own_scale, other_scale]),
            jnp.concatenate([other_scale, own_scale]),
        ),
        col * block,
        block,
    )[:, None]
    outs, peaks = [], []
    for group in GROUPS:
        total = jnp.concatenate([totals[at] for at in group], axis=1)
        for at in range(1, bits):
            middle = total.shape[0] // 2
            got = stage(total[middle:].astype(jnp.bfloat16), at)
            keep = total[:middle]
            if at < bits - 1:
                total = keep + got.astype(jnp.float32)
        out, top = finish(keep, got, mine, amax_history)
        outs.append(out)
        peaks.append(top)

    newest = functools.reduce(jnp.maximum, peaks)
    flips = [(1, 0)] + [(0, 1 << bit) for bit in range(bits)]
    for at in range(0, len(flips), 2):
        (ar, ac), *more = flips[at : at + 2]
        near = [(ar, ac)]
        for br, bc in more:
            near += [(br, bc), (ar ^ br, ac ^ bc)]
        newest = functools.reduce(
            jnp.maximum, [newest] + [across(newest, both(*flip)) for flip in near]
        )
    history_next = jnp.concatenate([newest[0, :1], amax_history[:-1]])
    return (jnp.concatenate(outs, axis=1), own_scale, history_next)


def solution(mesh):
    in_specs = (P(("grp", "row"), "col"), P("col", "row"), P("grp"))
    out_specs = (P(("grp", "col"), "row"), P(("grp", "row")), P("grp"))
    return jax.shard_map(
        on_device, mesh=mesh, in_specs=in_specs, out_specs=out_specs, check_vma=False
    )
```

```python
import functools

import jax
import jax.numpy as jnp
from jax import lax
from jax.experimental import pallas as pl
from jax.experimental.pallas import tpu as pltpu
from jax.sharding import PartitionSpec as P


clip_ratio = 0.5
format_limit = 448.0
EIGHTHS = (1, 2, 3, 2)
GROUPS = ((0, 1), (2, 3))


def orders_of(bits):
    orders = [list(range(bits)), list(range(bits))]
    if bits > 1:
        orders[1][:2] = [1, 0]
    return orders


def matmul(lhs_ref, weight_ref, keep_ref, send_ref):
    half, width = keep_ref.shape
    tile = min(512, width)

    @pl.loop(0, width // tile)
    def _(step):
        at = pl.ds(pl.multiple_of(step * tile, tile), tile)
        out = jnp.dot(
            lhs_ref[...], weight_ref[:, at], preferred_element_type=jnp.float32
        )
        keep_ref[:, at] = out[:half]
        send_ref[:, at] = out[half:].astype(jnp.bfloat16)


def first_body(
    cols,
    own_hbm,
    other_ref,
    own_scale,
    other_scale,
    weight_hbm,
    lhs_ref,
    keep_ref,
    send_ref,
    next_ref,
    own_ref,
    weight_ref,
    sems,
):
    bits = cols.bit_length() - 1
    orders = orders_of(bits)
    col, row = lax.axis_index("col"), lax.axis_index("row")
    half = cols // 2
    size = lhs_ref.shape[0] // cols
    width, after = weight_ref.shape[1], next_ref.shape[1]
    own_copy = pltpu.make_async_copy(own_hbm, own_ref, sems.at[0])
    own_copy.start()
    now = pltpu.make_async_copy(weight_hbm.at[:, :width], weight_ref, sems.at[1])
    now.start()

    def position(block):
        away = block ^ col
        where = [
            sum(((away >> bit) & 1) << (bits - 1 - j) for j, bit in enumerate(order))
            for order in orders
        ]
        return jnp.where(row == 0, where[0], where[1])

    def quantize(acts_ref, scale_ref, owner):
        @pl.loop(0, half)
        def _(step):
            at = pl.ds(pl.multiple_of(step * size, size), size)
            to = pl.ds(pl.multiple_of(position(owner * half + step) * size, size), size)
            inverse = 1.0 / scale_ref[at, :]
            values = acts_ref[at, :].astype(jnp.float32) * inverse
            lhs_ref[to, :] = jnp.clip(values, -format_limit, format_limit).astype(
                jnp.bfloat16
            )

    quantize(other_ref, other_scale, 1 - row)
    own_copy.wait()
    later = pltpu.make_async_copy(
        weight_hbm.at[:, width : width + after], next_ref, sems.at[2]
    )
    later.start()
    quantize(own_ref, own_scale, row)
    now.wait()
    matmul(lhs_ref, weight_ref, keep_ref, send_ref)
    later.wait()


def middle_body(
    begin, lhs_ref, weight_ref, weight_hbm, keep_ref, send_ref, next_ref, sem
):
    after = next_ref.shape[1]
    later = pltpu.make_async_copy(
        weight_hbm.at[:, begin : begin + after], next_ref, sem
    )
    later.start()
    matmul(lhs_ref, weight_ref, keep_ref, send_ref)
    later.wait()


def last_body(lhs_ref, weight_ref, keep_ref, send_ref):
    matmul(lhs_ref, weight_ref, keep_ref, send_ref)


def finish_body(history, keep_ref, got_ref, scale_ref, out_ref, peak_ref):
    result = (keep_ref[...] + got_ref[...].astype(jnp.float32)) * scale_ref[...]
    previous = history[0]
    for at in range(1, history.shape[0]):
        previous = jnp.maximum(previous, history[at])
    out_ref[...] = jnp.clip(result / previous, -1.0, 1.0).astype(jnp.bfloat16)
    peak_ref[...] = jnp.full(peak_ref.shape, jnp.max(jnp.abs(result)), jnp.float32)


VMEM = pl.BlockSpec(memory_space=pltpu.VMEM)
SMEM = pl.BlockSpec(memory_space=pltpu.SMEM)
HBM = pl.BlockSpec(memory_space=pltpu.HBM)


def products(own, other, own_scale, other_scale, weight, cols):
    rows, depth = own.shape
    total = 2 * rows
    widths = [weight.shape[1] * part // sum(EIGHTHS) for part in EIGHTHS]
    pair = lambda width: (
        jax.ShapeDtypeStruct((total // 2, width), jnp.float32),
        jax.ShapeDtypeStruct((total // 2, width), jnp.bfloat16),
    )
    piece = lambda width: pltpu.VMEM((depth, width), jnp.bfloat16)
    params = pltpu.CompilerParams(vmem_limit_bytes=12 << 20)
    cost = lambda width: pl.CostEstimate(
        flops=2 * total * depth * width,
        bytes_accessed=2 * depth * width,
        transcendentals=0,
    )
    lhs, *first, held = pl.pallas_call(
        functools.partial(first_body, cols),
        out_shape=(
            jax.ShapeDtypeStruct((total, depth), jnp.bfloat16),
            *pair(widths[0]),
            piece(widths[1]),
        ),
        in_specs=[HBM, VMEM, VMEM, VMEM, HBM],
        out_specs=(VMEM,) * 4,
        scratch_shapes=[
            pltpu.VMEM((rows, depth), jnp.bfloat16),
            pltpu.VMEM((depth, widths[0]), jnp.bfloat16),
            pltpu.SemaphoreType.DMA((3,)),
        ],
        compiler_params=params,
        cost_estimate=cost(widths[0]),
        name="first",
    )(own, other, own_scale, other_scale, weight)
    made = [first]
    begin = widths[0]
    for at in range(1, len(widths)):
        begin += widths[at]
        if at + 1 < len(widths):
            *part, held = pl.pallas_call(
                functools.partial(middle_body, begin),
                out_shape=(*pair(widths[at]), piece(widths[at + 1])),
                in_specs=[VMEM, VMEM, HBM],
                out_specs=(VMEM,) * 3,
                scratch_shapes=[pltpu.SemaphoreType.DMA],
                compiler_params=params,
                cost_estimate=cost(widths[at]),
                name="middle",
            )(lhs, held, weight)
        else:
            part = pl.pallas_call(
                last_body,
                out_shape=pair(widths[at]),
                in_specs=[VMEM, VMEM],
                out_specs=(VMEM,) * 2,
                compiler_params=params,
                cost_estimate=cost(widths[at]),
                name="last",
            )(lhs, held)
        made.append(part)
    return made


def finish(keep, got, scale, history):
    return pl.pallas_call(
        finish_body,
        out_shape=(
            jax.ShapeDtypeStruct(keep.shape, jnp.bfloat16),
            jax.ShapeDtypeStruct((8, 128), jnp.float32),
        ),
        in_specs=[SMEM, VMEM, VMEM, VMEM],
        out_specs=(VMEM, VMEM),
        compiler_params=pltpu.CompilerParams(vmem_limit_bytes=8 << 20),
        cost_estimate=pl.CostEstimate(
            flops=6 * keep.size, bytes_accessed=6 * keep.size, transcendentals=0
        ),
        name="finish",
    )(history, keep, got, scale)


def on_device(hidden_acts, down_weight, amax_history):
    cols = lax.axis_size("col")
    bits = cols.bit_length() - 1
    orders = orders_of(bits)
    col, row = lax.axis_index("col"), lax.axis_index("row")
    block = 2 * hidden_acts.shape[0] // cols

    def across(value, flips):
        pairs = []
        for r in range(2):
            for c in range(cols):
                dr, dc = flips[r]
                pairs.append((r * cols + c, (r ^ dr) * cols + (c ^ dc)))
        return lax.ppermute(value, ("row", "col"), pairs)

    def both(dr, dc):
        return ((dr, dc), (dr, dc))

    def stage(value, at):
        return across(value, tuple((0, 1 << orders[r][at]) for r in range(2)))

    weight = pltpu.with_memory_space_constraint(down_weight, pltpu.HBM)
    own_acts = pltpu.with_memory_space_constraint(hidden_acts, pltpu.HBM)
    other_acts = across(hidden_acts, both(1, 0))
    peak = jnp.max(jnp.abs(hidden_acts), axis=1).astype(jnp.float32)
    for bit in range(bits):
        peak = jnp.maximum(peak, across(peak, both(0, 1 << bit)))
    own_scale = clip_ratio * (peak + 1e-06) / format_limit
    other_scale = across(own_scale, both(1, 0))

    made = products(
        own_acts, other_acts, own_scale[:, None], other_scale[:, None], weight, cols
    )
    totals = []
    for keep, send in made:
        got = stage(send, 0)
        totals.append(keep + got.astype(jnp.float32))

    mine = lax.dynamic_slice_in_dim(
        jnp.where(
            row == 0,
            jnp.concatenate([own_scale, other_scale]),
            jnp.concatenate([other_scale, own_scale]),
        ),
        col * block,
        block,
    )[:, None]
    outs, peaks = [], []
    for group in GROUPS:
        total = jnp.concatenate([totals[at] for at in group], axis=1)
        for at in range(1, bits):
            middle = total.shape[0] // 2
            got = stage(total[middle:].astype(jnp.bfloat16), at)
            keep = total[:middle]
            if at < bits - 1:
                total = keep + got.astype(jnp.float32)
        out, top = finish(keep, got, mine, amax_history)
        outs.append(out)
        peaks.append(top)

    newest = functools.reduce(jnp.maximum, peaks)
    flips = [(1, 0)] + [(0, 1 << bit) for bit in range(bits)]
    for at in range(0, len(flips), 2):
        (ar, ac), *more = flips[at : at + 2]
        near = [(ar, ac)]
        for br, bc in more:
            near += [(br, bc), (ar ^ br, ac ^ bc)]
        newest = functools.reduce(
            jnp.maximum, [newest] + [across(newest, both(*flip)) for flip in near]
        )
    history_next = jnp.concatenate([newest[0, :1], amax_history[:-1]])
    return (jnp.concatenate(outs, axis=1), own_scale, history_next)


def solution(mesh):
    in_specs = (P(("grp", "row"), "col"), P("col", "row"), P("grp"))
    out_specs = (P(("grp", "col"), "row"), P(("grp", "row")), P("grp"))
    return jax.shard_map(
        on_device, mesh=mesh, in_specs=in_specs, out_specs=out_specs, check_vma=False
    )
```

```python
import functools

import jax
import jax.numpy as jnp
from jax import lax
from jax.experimental import pallas as pl
from jax.experimental.pallas import tpu as pltpu
from jax.sharding import PartitionSpec as P


clip_ratio = 0.5
format_limit = 448.0
PARTS = (4, 6, 4, 2)
GROUPS = ((0, 1), (2,), (3,))
FIRST = (((0, 1), (1, 0)), ((0, 1), (1, 0)), ((0, 1), (1, 0)))
AHEAD = 512


def order_of(chunk, row, bits):
    group = next(at for at, group in enumerate(GROUPS) if chunk in group)
    first = [bit for bit in FIRST[group][row] if bit < bits]
    return first + [bit for bit in range(bits) if bit not in first]


def tiles_of(width):
    edges = [*range(0, width, min(AHEAD, width)), width]
    return list(zip(edges, edges[1:]))


def matmul(chunk, cols, columns, lhs_ref, weight, keep_ref, send_ref):
    half = keep_ref.shape[0]
    size = 2 * half // cols
    bits = cols.bit_length() - 1
    row = lax.axis_index("row")
    out = jnp.dot(lhs_ref[...], weight, preferred_element_type=jnp.float32)

    def store(mine):
        order = order_of(chunk, mine, bits)
        for away in range(cols):
            place = size * sum(
                ((away >> bit) & 1) << (bits - 1 - j) for j, bit in enumerate(order)
            )
            part = out[away * size : (away + 1) * size]
            if place < half:
                keep_ref[place : place + size, columns] = part
            else:
                send_ref[place - half : place - half + size, columns] = part.astype(
                    jnp.bfloat16
                )

    if order_of(chunk, 0, bits) == order_of(chunk, 1, bits):
        store(0)
    else:
        for mine in range(2):
            pl.when(row == mine)(functools.partial(store, mine))


def chunk_body(chunk, cols, begin, head, fetches, lhs_ref, keep_ref, send_ref, rest, sems):
    width = keep_ref.shape[1]
    first, *others = tiles_of(width)
    weight_hbm, prepare, later = fetches
    copies = [
        pltpu.make_async_copy(
            weight_hbm.at[:, begin + low : begin + high],
            rest.at[:, low - first[1] : high - first[1]],
            sems.at[at],
        )
        for at, (low, high) in enumerate(others)
    ]
    queue = copies + later
    for copy in queue[:2]:
        copy.start()
    prepare()
    matmul(chunk, cols, slice(*first), lhs_ref, head[...], keep_ref, send_ref)
    for at, (low, high) in enumerate(others):
        queue[at].wait()
        for copy in queue[at + 2 : at + 3]:
            copy.start()
        part = rest[:, low - first[1] : high - first[1]]
        matmul(chunk, cols, slice(low, high), lhs_ref, part, keep_ref, send_ref)
    for copy in later:
        copy.wait()


def first_body(
    cols,
    own_hbm,
    other_ref,
    own_scale,
    other_scale,
    weight_hbm,
    lhs_ref,
    keep_ref,
    send_ref,
    next_ref,
    own_ref,
    head_ref,
    rest_ref,
    sems,
):
    col, row = lax.axis_index("col"), lax.axis_index("row")
    half = cols // 2
    size = lhs_ref.shape[0] // cols
    width = keep_ref.shape[1]
    head, ahead = head_ref.shape[1], next_ref.shape[1]
    own_copy = pltpu.make_async_copy(own_hbm, own_ref, sems.at[0])
    own_copy.start()
    now = pltpu.make_async_copy(weight_hbm.at[:, :head], head_ref, sems.at[1])
    now.start()
    later = pltpu.make_async_copy(
        weight_hbm.at[:, width : width + ahead], next_ref, sems.at[2]
    )

    def quantize(acts_ref, scale_ref, owner):
        @pl.loop(0, half)
        def _(step):
            at = pl.ds(pl.multiple_of(step * size, size), size)
            to = pl.ds(pl.multiple_of(((owner * half + step) ^ col) * size, size), size)
            inverse = 1.0 / scale_ref[at, :]
            values = acts_ref[at, :].astype(jnp.float32) * inverse
            lhs_ref[to, :] = jnp.clip(values, -format_limit, format_limit).astype(
                jnp.bfloat16
            )

    def prepare():
        quantize(other_ref, other_scale, 1 - row)
        own_copy.wait()
        quantize(own_ref, own_scale, row)
        now.wait()

    chunk_body(
        0,
        cols,
        0,
        head_ref,
        (weight_hbm, prepare, [later]),
        lhs_ref,
        keep_ref,
        send_ref,
        rest_ref,
        sems.at[pl.ds(3, sems.shape[0] - 3)],
    )


def later_body(
    chunk,
    cols,
    begin,
    lhs_ref,
    head_ref,
    weight_hbm,
    keep_ref,
    send_ref,
    *refs,
):
    *next_refs, rest_ref, sems = refs
    after = begin + keep_ref.shape[1]
    later = [
        pltpu.make_async_copy(
            weight_hbm.at[:, after : after + next_ref.shape[1]], next_ref, sems.at[0]
        )
        for next_ref in next_refs
    ]
    chunk_body(
        chunk,
        cols,
        begin,
        head_ref,
        (weight_hbm, lambda: None, later),
        lhs_ref,
        keep_ref,
        send_ref,
        rest_ref,
        sems.at[pl.ds(1, sems.shape[0] - 1)],
    )


def finish_body(history, keep_ref, got_ref, scale_ref, out_ref, peak_ref):
    result = (keep_ref[...] + got_ref[...].astype(jnp.float32)) * scale_ref[...]
    previous = jnp.max(history[...])
    out_ref[...] = jnp.clip(result / previous, -1.0, 1.0).astype(jnp.bfloat16)
    peak_ref[...] = jnp.full(peak_ref.shape, jnp.max(jnp.abs(result)), jnp.float32)


VMEM = pl.BlockSpec(memory_space=pltpu.VMEM)
HBM = pl.BlockSpec(memory_space=pltpu.HBM)


def products(own, other, own_scale, other_scale, weight, cols):
    rows, depth = own.shape
    total = 2 * rows
    widths = [weight.shape[1] * part // sum(PARTS) for part in PARTS]
    params = pltpu.CompilerParams(vmem_limit_bytes=20 << 20)
    piece = lambda width: pltpu.VMEM((depth, width), jnp.bfloat16)
    head = lambda width: tiles_of(width)[0][1]

    def rest(width):
        return [piece(max(width - head(width), 128))]

    made = []
    for at, width in enumerate(widths):
        common = dict(
            compiler_params=params,
            cost_estimate=pl.CostEstimate(
                flops=2 * total * depth * width,
                bytes_accessed=2 * depth * width,
                transcendentals=0,
            ),
        )
        pair = (
            jax.ShapeDtypeStruct((rows, width), jnp.float32),
            jax.ShapeDtypeStruct((rows, width), jnp.bfloat16),
        )
        ahead = [piece(head(after)) for after in widths[at + 1 : at + 2]]
        tiles = len(tiles_of(width))
        if at == 0:
            lhs, *part = pl.pallas_call(
                functools.partial(first_body, cols),
                out_shape=(
                    jax.ShapeDtypeStruct((total, depth), jnp.bfloat16),
                    *pair,
                    *ahead,
                ),
                in_specs=[HBM, VMEM, VMEM, VMEM, HBM],
                out_specs=(VMEM,) * 4,
                scratch_shapes=[
                    pltpu.VMEM((rows, depth), jnp.bfloat16),
                    piece(head(width)),
                    *rest(width),
                    pltpu.SemaphoreType.DMA((3 + tiles,)),
                ],
                name="first",
                **common,
            )(own, other, own_scale, other_scale, weight)
        else:
            part = pl.pallas_call(
                functools.partial(later_body, at, cols, sum(widths[:at])),
                out_shape=(*pair, *ahead),
                in_specs=[VMEM, VMEM, HBM],
                out_specs=(VMEM,) * (2 + len(ahead)),
                scratch_shapes=[*rest(width), pltpu.SemaphoreType.DMA((1 + tiles,))],
                name="later",
                **common,
            )(lhs, *held, weight)
        made.append(part[:2])
        held = part[2:]
    return made


def finish(keep, got, scale, history):
    return pl.pallas_call(
        finish_body,
        out_shape=(
            jax.ShapeDtypeStruct(keep.shape, jnp.bfloat16),
            jax.ShapeDtypeStruct((8, 128), jnp.float32),
        ),
        in_specs=[VMEM, VMEM, VMEM, VMEM],
        out_specs=(VMEM, VMEM),
        compiler_params=pltpu.CompilerParams(vmem_limit_bytes=8 << 20),
        cost_estimate=pl.CostEstimate(
            flops=6 * keep.size, bytes_accessed=6 * keep.size, transcendentals=0
        ),
        name="finish",
    )(history[None, :], keep, got, scale)


def on_device(hidden_acts, down_weight, amax_history):
    cols = lax.axis_size("col")
    bits = cols.bit_length() - 1
    col, row = lax.axis_index("col"), lax.axis_index("row")
    block = 2 * hidden_acts.shape[0] // cols

    def across(value, flips):
        pairs = []
        for r in range(2):
            for c in range(cols):
                dr, dc = flips[r]
                pairs.append((r * cols + c, (r ^ dr) * cols + (c ^ dc)))
        return lax.ppermute(value, ("row", "col"), pairs)

    def both(dr, dc):
        return ((dr, dc), (dr, dc))

    def stage(value, chunk, at):
        return across(
            value, tuple((0, 1 << order_of(chunk, r, bits)[at]) for r in range(2))
        )

    weight = pltpu.with_memory_space_constraint(down_weight, pltpu.HBM)
    own_acts = pltpu.with_memory_space_constraint(hidden_acts, pltpu.HBM)
    other_acts = across(hidden_acts, both(1, 0))
    peak = jnp.max(jnp.abs(hidden_acts), axis=1).astype(jnp.float32)
    for bit in range(bits - 1):
        got = across(peak, both(0, 1 << bit))
        peak = jnp.maximum(peak, got)
    far = 1 << (bits - 1)
    row_got, far_got, both_got = (
        across(peak, both(*flips)) for flips in ((1, 0), (0, far), (1, far))
    )
    own_scale = clip_ratio * (jnp.maximum(peak, far_got) + 1e-06) / format_limit
    other_scale = clip_ratio * (jnp.maximum(row_got, both_got) + 1e-06) / format_limit

    made = products(
        own_acts, other_acts, own_scale[:, None], other_scale[:, None], weight, cols
    )
    totals = []
    for at, (keep, send) in enumerate(made):
        totals.append((keep, stage(send, at, 0)))

    mine = lax.dynamic_slice_in_dim(
        jnp.where(
            row == 0,
            jnp.concatenate([own_scale, other_scale]),
            jnp.concatenate([other_scale, own_scale]),
        ),
        col * block,
        block,
    )[:, None]
    outs, peaks, before = [], [], None
    for group in GROUPS:
        parts = []
        for at in group:
            keep, got = totals[at]
            if before is not None:
                keep, _ = lax.optimization_barrier((keep, before))
            parts.append(keep + got.astype(jnp.float32))
        total = jnp.concatenate(parts, axis=1)
        for at in range(1, bits):
            middle = total.shape[0] // 2
            send = total[middle:].astype(jnp.bfloat16)
            if at == 1:
                before = send
            got = stage(send, group[0], at)
            keep = total[:middle]
            if at < bits - 1:
                total = keep + got.astype(jnp.float32)
        out, top = finish(keep, got, mine, amax_history)
        outs.append(out)
        peaks.append(top)

    newest = functools.reduce(jnp.maximum, peaks)
    flips = [(1, 0)] + [(0, 1 << bit) for bit in range(bits)]
    for at in range(0, len(flips), 2):
        (ar, ac), *more = flips[at : at + 2]
        near = [(ar, ac)]
        for br, bc in more:
            near += [(br, bc), (ar ^ br, ac ^ bc)]
        newest = functools.reduce(
            jnp.maximum, [newest] + [across(newest, both(*flip)) for flip in near]
        )
    entries = amax_history.shape[0]
    history_next = jnp.where(
        lax.iota(jnp.int32, entries) == 0,
        newest[0, :entries],
        jnp.concatenate([amax_history[:1], amax_history[:-1]]),
    )
    return (jnp.concatenate(outs, axis=1), own_scale, history_next)


def solution(mesh):
    in_specs = (P(("grp", "row"), "col"), P("col", "row"), P("grp"))
    out_specs = (P(("grp", "col"), "row"), P(("grp", "row")), P("grp"))
    return jax.shard_map(
        on_device, mesh=mesh, in_specs=in_specs, out_specs=out_specs, check_vma=False
    )
```
